32 devices in a mesh: rep: 16 (over z, x, core), shard: 2 (over y).
Axes of the slice: x: 2, y: 2, z: 4, core: 2. Of those that a mesh axis runs over, the one named last changes fastest.
Arguments:
- tokens: bfloat16 [16, 1024, 768], P('rep', 'shard'), may hold values from -6 to 6
- cotangent: bfloat16 [16, 1024, 768], P('rep', 'shard'), may hold values from -6 to 6
- gain_attention: bfloat16 [2, 768], P(None, 'shard'), may hold values from 0.099609375 to 1.8984375
- heads_in: bfloat16 [2, 768, 2304], P(None, 'shard'), may hold values from -0.21875 to 0.21875
- heads_out: bfloat16 [2, 768, 768], P(None, 'shard'), may hold values from -2.5 to 2.5
- gain_feedforward: bfloat16 [2, 768], P(None, 'shard'), may hold values from 0.099609375 to 1.8984375
- expand_in: bfloat16 [2, 768, 2304], P(None, 'shard'), may hold values from -0.21875 to 0.21875
- reduce_out: bfloat16 [2, 1152, 768], P(None, 'shard'), may hold values from -0.25 to 0.25
Outputs:
- output: bfloat16 [16, 1024, 768], P('rep', 'shard')
- input_grad: float32 [16, 1024, 768], P('rep', 'shard')
- gain_attention_grad: float32 [2, 768], P(None, 'shard')
- heads_in_grad: float32 [2, 768, 2304], P(None, 'shard')
- heads_out_grad: float32 [2, 768, 768], P(None, 'shard')
- gain_feedforward_grad: float32 [2, 768], P(None, 'shard')
- expand_in_grad: float32 [2, 768, 2304], P(None, 'shard')
- reduce_out_grad: float32 [2, 1152, 768], P(None, 'shard')
The draws below stay inside these ranges and needn't reach their ends.
All inputs are finite; a program needn't handle non-finite values.
Results may differ from the reference program's by a relative error of at most 0.025.
Values may be sent and summed in bfloat16 or wider, within the bound.
No kernel may reach another device: no remote copies, remote signals or barrier semaphores. Data moves between devices by JAX's collectives and lax.ppermute only.
A program may use at most 192 MiB of HBM per device.

```python
import math
import jax
import jax.numpy as jnp
from jax import lax

D = 768
HEADS = 12
HDIM = 64
FF = 1152
HALF = 64
LAYERS = 2
LENGTH = 1024
BATCH = 16


def steps_of(rng, extent, pieces, least, high):
    def one(axis_at, blocks):
        steps = jax.random.uniform(jax.random.fold_in(jax.random.fold_in(rng, 6), axis_at), (blocks,), jnp.float32, least / len(pieces), high / len(pieces))
        return jnp.repeat(jnp.exp(steps), extent[axis_at] // blocks).reshape((-1,) + (1,) * (len(extent) - axis_at - 1))

    level = one(*pieces[0])
    for cut in pieces[1:]:
        level = level * one(*cut)
    return level


def normal_values(own_key, extent, width, most, pieces=(), kind=jnp.bfloat16):
    drawn = width * jax.random.normal(own_key, extent, jnp.float32)
    if pieces:
        drawn = drawn * steps_of(own_key, extent, pieces, -0.22, 0.18)
    return jnp.clip(drawn, -most, most).astype(kind)


def setup_inputs(seed: int = 0) -> dict:
    keys = jax.random.split(jax.random.key(seed), 9)
    tokens = normal_values(keys[0], (BATCH, LENGTH, D), 1.0, 6.0, ((0, 16), (1, 2)))
    cotangent = normal_values(keys[1], (BATCH, LENGTH, D), 1.0, 6.0, ((0, 16), (1, 2)))
    gain_attention = jnp.clip(1.0 + 0.18 * jax.random.normal(keys[2], (LAYERS, D), jnp.float32), 0.099609375, 1.8984375).astype(jnp.bfloat16)
    heads_in = normal_values(keys[3], (LAYERS, D, 3 * D), D ** -0.5, 0.21875, ((1, 2),))
    heads_out = normal_values(keys[4], (LAYERS, D, D), (max(D // 128, 4)) ** -0.5, 2.5, ((1, 2),))
    gain_feedforward = jnp.clip(1.0 + 0.18 * jax.random.normal(keys[5], (LAYERS, D), jnp.float32), 0.099609375, 1.8984375).astype(jnp.bfloat16)
    expand_in = normal_values(keys[6], (LAYERS, D, 2 * FF), D ** -0.5, 0.21875, ((1, 2),))
    reduce_out = normal_values(keys[7], (LAYERS, FF, D), (FF // 2) ** -0.5, 0.25, ((1, 2),))
    return dict(tokens=tokens, cotangent=cotangent, gain_attention=gain_attention, heads_in=heads_in, heads_out=heads_out, gain_feedforward=gain_feedforward, expand_in=expand_in, reduce_out=reduce_out)


@jax.custom_vjp
def low(v):
    return lax.optimization_barrier(v.astype(jnp.bfloat16)).astype(jnp.float32)

@jax.custom_vjp
def low_back(v):
    return v

def low_keep(v):
    return (low(v), None)

def low_pass(kept, grad):
    return (grad,)

def back_keep(v):
    return (v, None)

def back_low(kept, grad):
    return (low(grad),)
low.defvjp(low_keep, low_pass)
low_back.defvjp(back_keep, back_low)
PRECISE = lax.Precision.HIGHEST
MASKED_SCORE = -1e+30

def layer_norm(value, gain):
    center = lax.optimization_barrier(jnp.mean(value, axis=-1, keepdims=True))
    centered = value - center
    spread = lax.optimization_barrier(jnp.mean(centered * centered, axis=-1, keepdims=True))
    return centered * lax.rsqrt(spread + 1e-05) * gain

def rope_tables(positions, head_size):
    half_size = head_size // 2
    freqs = jnp.exp(jnp.arange(half_size, dtype=jnp.float32) * (-2.0 * math.log(10000.0) / head_size))
    angles = positions.astype(jnp.float32)[:, None] * freqs[None, :]
    angles = jnp.concatenate([angles, angles], axis=-1)
    return (jnp.cos(angles), jnp.sin(angles))

def rotate(value, cosine, sine):
    half_size = value.shape[-1] // 2
    turned = jnp.concatenate([-value[..., half_size:], value[..., :half_size]], axis=-1)
    return value * cosine[:, None, :] + turned * sine[:, None, :]

def into_blocks(extended, block_count, block_rows, key_span):
    return jnp.stack([extended[:, n * block_rows:n * block_rows + key_span] for n in range(block_count)], axis=1)

def build_mask(offset, local_length, length_all):
    block_rows = 2 * HALF
    key_span = 4 * HALF
    block_count = local_length // block_rows
    query_idx = jnp.arange(block_rows, dtype=jnp.int32)[:, None]
    key_idx = jnp.arange(key_span, dtype=jnp.int32)[None, :]
    block_num = jnp.arange(block_count, dtype=jnp.int32)[:, None, None]
    key_pos = offset + block_num * block_rows + key_idx - HALF
    near = jnp.abs(query_idx - key_idx + HALF) <= HALF
    inside = (key_pos >= 0) & (key_pos < length_all)
    return (near & inside)[:, None]

def layer(stream, gain_one, weight_qkv, weight_out, gain_two, weight_in, weight_down, cosine, sine, window_mask):
    sequences = stream.shape[0]
    normed = low(layer_norm(stream, gain_one))
    mixed = low_back(jnp.einsum('std,de->ste', normed, weight_qkv, precision=PRECISE))
    mixed = mixed.reshape(sequences, LENGTH, 3, HEADS, HDIM)
    queries = low(rotate(mixed[:, :, 0], cosine, sine))
    key_rows = low(rotate(mixed[:, :, 1], cosine, sine))
    value_rows = low(mixed[:, :, 2])
    block_rows = 2 * HALF
    key_span = 4 * HALF
    block_count = LENGTH // block_rows
    padding = ((0, 0), (HALF, HALF), (0, 0), (0, 0))
    key_blocks = into_blocks(jnp.pad(key_rows, padding), block_count, block_rows, key_span)
    value_blocks = into_blocks(jnp.pad(value_rows, padding), block_count, block_rows, key_span)
    query_blocks = queries.reshape(sequences, block_count, block_rows, HEADS, HDIM)
    scores = jnp.einsum('snqhd,snkhd->snhqk', query_blocks, key_blocks, precision=PRECISE) * (1.0 / math.sqrt(HDIM))
    scores = low_back(scores)
    scores = jnp.where(window_mask, scores, MASKED_SCORE)
    probability = low(jax.nn.softmax(scores, axis=-1))
    attended = jnp.einsum('snhqk,snkhd->snqhd', probability, value_blocks, precision=PRECISE)
    attended = low_back(low(attended.reshape(sequences, LENGTH, D)))
    middle = stream + low_back(jnp.einsum('std,de->ste', attended, weight_out, precision=PRECISE))
    normed_two = low(layer_norm(middle, gain_two))
    gate_up = low_back(jnp.einsum('std,de->ste', normed_two, weight_in, precision=PRECISE))
    hidden = low(jax.nn.gelu(gate_up[..., :FF], approximate=False) * gate_up[..., FF:])
    return middle + low_back(jnp.einsum('stf,fd->std', hidden, weight_down, precision=PRECISE))

def forward(stream, params, cosine, sine, window_mask):
    gain_attention, heads_in, heads_out, gain_feedforward, expand_in, reduce_out = params
    for layer_num in range(LAYERS):
        stream = layer(stream, gain_attention[layer_num], heads_in[layer_num], heads_out[layer_num], gain_feedforward[layer_num], expand_in[layer_num], reduce_out[layer_num], cosine, sine, window_mask)
    return stream

def reference(tokens, cotangent, gain_attention, heads_in, heads_out, gain_feedforward, expand_in, reduce_out):
    params = tuple((w.astype(jnp.float32) for w in (gain_attention, heads_in, heads_out, gain_feedforward, expand_in, reduce_out)))
    cosine, sine = rope_tables(jnp.arange(LENGTH, dtype=jnp.int32), HDIM)
    window_mask = build_mask(0, LENGTH, LENGTH)
    group = math.gcd(BATCH, max(1, 4096 // LENGTH))
    inputs = tokens.astype(jnp.float32).reshape(BATCH // group, group, LENGTH, D)
    cots = cotangent.astype(jnp.float32).reshape(BATCH // group, group, LENGTH, D)

    def step_group(totals, pair):
        values_in, cot_in = pair

        def whole(xv, *pv):
            return forward(xv, pv, cosine, sine, window_mask)
        result, pull = jax.vjp(whole, values_in, *params)
        grads_all = pull(cot_in)
        totals = tuple((t + g for t, g in zip(totals, grads_all[1:])))
        return (totals, (result.astype(jnp.bfloat16), grads_all[0]))
    zeros = tuple((jnp.zeros_like(p) for p in params))
    totals, (results, input_grads) = lax.scan(step_group, zeros, (inputs, cots))
    return (results.reshape(BATCH, LENGTH, D), input_grads.reshape(BATCH, LENGTH, D), totals[0], totals[1], totals[2], totals[3], totals[4], totals[5])
```

```python
import math

import jax
import jax.numpy as jnp
from jax import lax
from jax.sharding import Mesh
from jax.sharding import PartitionSpec as P

HEADS = 12
HDIM = 64
HALF = 64


MASKED_SCORE = -1e30
EPSILON = 1e-05


def with_halo(x, sides, width):
    for axis, dim in sides:
        count, length = (lax.axis_size(axis), x.shape[dim])
        up = [(i, (i + 1) % count) for i in range(count - 1)]
        down = [(j, i) for i, j in up]
        last = lax.slice_in_dim(x, length - width, length, axis=dim)
        first = lax.slice_in_dim(x, 0, width, axis=dim)
        before = lax.ppermute(last, axis, up)
        after = lax.ppermute(first, axis, down)
        x = jnp.concatenate([before, x, after], axis=dim)
    return x


def shifted(block, axis, distance):
    devices = range(lax.axis_size(axis))
    route = [(i - distance, i) for i in devices if i - distance in devices]
    return lax.ppermute(block, axis, route)


def normalize(value):
    center = jnp.mean(value, axis=-1, keepdims=True)
    centered = value - center
    inverse = lax.rsqrt(jnp.mean(centered * centered, axis=-1, keepdims=True) + EPSILON)
    return (centered * inverse, inverse)


def norm_back(grad_norm, normed, inverse):
    return inverse * (
        grad_norm
        - jnp.mean(grad_norm, axis=-1, keepdims=True)
        - normed * jnp.mean(grad_norm * normed, axis=-1, keepdims=True)
    )


def rope_tables(positions, head_size):
    half_size = head_size // 2
    freqs = jnp.exp(
        jnp.arange(half_size, dtype=jnp.float32) * (-2.0 * math.log(10000.0) / head_size)
    )
    angles = positions.astype(jnp.float32)[:, None] * freqs[None, :]
    angles = jnp.concatenate([angles, angles], axis=-1)
    return (jnp.cos(angles), jnp.sin(angles))


def rotate(value, cosine, sine):
    half_size = value.shape[-1] // 2
    turned = jnp.concatenate([-value[..., half_size:], value[..., :half_size]], axis=-1)
    return value * cosine[:, None, :] + turned * sine[:, None, :]


def rotate_back(gradient, cosine, sine):
    half_size = gradient.shape[-1] // 2
    scaled = gradient * sine[:, None, :]
    return gradient * cosine[:, None, :] + jnp.concatenate(
        [scaled[..., half_size:], -scaled[..., :half_size]], axis=-1
    )


def into_blocks(extended, block_count, block_rows, key_span):
    return jnp.stack(
        [extended[:, n * block_rows : n * block_rows + key_span] for n in range(block_count)],
        axis=1,
    )


def from_blocks(blocked, block_count, block_rows, key_span, total_rows):
    summed = jnp.zeros(blocked.shape[:1] + (total_rows,) + blocked.shape[3:], blocked.dtype)
    for n in range(block_count):
        summed = summed.at[:, n * block_rows : n * block_rows + key_span].add(blocked[:, n])
    return summed


def build_mask(offset, local_length, length_all):
    block_rows = 2 * HALF
    key_span = 4 * HALF
    block_count = local_length // block_rows
    query_idx = jnp.arange(block_rows, dtype=jnp.int32)[:, None]
    key_idx = jnp.arange(key_span, dtype=jnp.int32)[None, :]
    block_num = jnp.arange(block_count, dtype=jnp.int32)[:, None, None]
    key_pos = offset + block_num * block_rows + key_idx - HALF
    near = jnp.abs(query_idx - key_idx + HALF) <= HALF
    inside = (key_pos >= 0) & (key_pos < length_all)
    return (near & inside)[:, None]


def weight_grad(left, right):
    return lax.dot_general(
        left, right, (((0,), (0,)), ((), ())), preferred_element_type=jnp.float32
    )


def back_dot(gradient, weight):
    return lax.dot_general(
        gradient, weight, (((1,), (1,)), ((), ())), preferred_element_type=jnp.float32
    )


def split_blocks(queries, extended):
    sequences, local_length, head_count, head_size = queries.shape
    model_width = head_count * head_size
    block_rows = 2 * HALF
    key_span = 4 * HALF
    block_count = local_length // block_rows
    query_blocks = queries.reshape(sequences, block_count, block_rows, head_count, head_size)
    key_blocks = into_blocks(extended[..., :model_width], block_count, block_rows, key_span)
    value_blocks = into_blocks(extended[..., model_width:], block_count, block_rows, key_span)
    key_blocks = key_blocks.reshape(sequences, block_count, key_span, head_count, head_size)
    value_blocks = value_blocks.reshape(sequences, block_count, key_span, head_count, head_size)
    return (query_blocks, key_blocks, value_blocks)


def masked_scores(query_blocks, key_blocks, window_mask):
    score_scale = 1.0 / math.sqrt(query_blocks.shape[-1])
    scores = (
        jnp.einsum(
            "snqhd,snkhd->snhqk", query_blocks, key_blocks, preferred_element_type=jnp.float32
        )
        * score_scale
    )
    return jnp.where(window_mask, scores, MASKED_SCORE)


def attend(queries, extended, window_mask):
    sequences, local_length, head_count, head_size = queries.shape
    query_blocks, key_blocks, value_blocks = split_blocks(queries, extended)
    scores = masked_scores(query_blocks, key_blocks, window_mask)
    row_max = jnp.max(scores, axis=-1, keepdims=True)
    exponent = jnp.exp(scores - row_max)
    row_sum = jnp.sum(exponent, axis=-1, keepdims=True)
    probability = (exponent / row_sum).astype(jnp.bfloat16)
    attended = jnp.einsum(
        "snhqk,snkhd->snqhd", probability, value_blocks, preferred_element_type=jnp.float32
    )
    return (
        attended.reshape(sequences, local_length, head_count * head_size),
        row_max + jnp.log(row_sum),
    )


def attend_back(queries, extended, log_total, grad_attended, window_mask):
    sequences, local_length, head_count, head_size = queries.shape
    model_width = head_count * head_size
    block_rows = 2 * HALF
    key_span = 4 * HALF
    block_count = local_length // block_rows
    score_scale = 1.0 / math.sqrt(head_size)
    query_blocks, key_blocks, value_blocks = split_blocks(queries, extended)
    scores = masked_scores(query_blocks, key_blocks, window_mask)
    probability = jnp.exp(scores - log_total)
    grad_blocks = grad_attended.reshape(sequences, block_count, block_rows, head_count, head_size)
    grad_prob = jnp.einsum(
        "snqhd,snkhd->snhqk", grad_blocks, value_blocks, preferred_element_type=jnp.float32
    )
    grad_values = jnp.einsum(
        "snhqk,snqhd->snkhd",
        probability.astype(jnp.bfloat16),
        grad_blocks,
        preferred_element_type=jnp.float32,
    )
    grad_scores = probability * (
        grad_prob - jnp.sum(probability * grad_prob, axis=-1, keepdims=True)
    )
    grad_scores = grad_scores.astype(jnp.bfloat16)
    grad_query = (
        jnp.einsum(
            "snhqk,snkhd->snqhd", grad_scores, key_blocks, preferred_element_type=jnp.float32
        )
        * score_scale
    )
    grad_keys = (
        jnp.einsum(
            "snhqk,snqhd->snkhd", grad_scores, query_blocks, preferred_element_type=jnp.float32
        )
        * score_scale
    )
    joined = jnp.concatenate(
        [
            grad_keys.reshape(sequences, block_count, key_span, model_width),
            grad_values.reshape(sequences, block_count, key_span, model_width),
        ],
        axis=-1,
    )
    grad_pair = from_blocks(joined, block_count, block_rows, key_span, local_length + 2 * HALF)
    return (grad_query.reshape(sequences, local_length, head_count, head_size), grad_pair)


def forward_layer(stream, gathered, cosine, sine, window_mask):
    gain_one, weight_qkv, weight_out, gain_two, weight_in, weight_down = gathered
    sequences, local_length, model_width = stream.shape
    row_count = sequences * local_length
    normed_one, inverse_one = normalize(stream)
    acts_one = (normed_one * gain_one.astype(jnp.float32)).astype(jnp.bfloat16)
    mixed = jnp.dot(
        acts_one.reshape(row_count, model_width), weight_qkv, preferred_element_type=jnp.float32
    )
    mixed = mixed.reshape(sequences, local_length, 3, HEADS, HDIM)
    queries = rotate(mixed[:, :, 0], cosine, sine).astype(jnp.bfloat16)
    key_rows = rotate(mixed[:, :, 1], cosine, sine).astype(jnp.bfloat16)
    value_rows = mixed[:, :, 2].astype(jnp.bfloat16)
    key_value = jnp.concatenate(
        [
            key_rows.reshape(sequences, local_length, model_width),
            value_rows.reshape(sequences, local_length, model_width),
        ],
        axis=-1,
    )
    extended = with_halo(key_value, (("shard", 1),), HALF)
    attended, log_total = attend(queries, extended, window_mask)
    attended_low = attended.astype(jnp.bfloat16).reshape(row_count, model_width)
    middle = stream + jnp.dot(attended_low, weight_out, preferred_element_type=jnp.float32).reshape(
        stream.shape
    )
    normed_two, inverse_two = normalize(middle)
    acts_two = (
        (normed_two * gain_two.astype(jnp.float32))
        .astype(jnp.bfloat16)
        .reshape(row_count, model_width)
    )
    gate_up = jnp.dot(acts_two, weight_in, preferred_element_type=jnp.float32)
    hidden_units = weight_down.shape[0]
    hidden = (
        jax.nn.gelu(gate_up[:, :hidden_units], approximate=False) * gate_up[:, hidden_units:]
    ).astype(jnp.bfloat16)
    result = middle + jnp.dot(hidden, weight_down, preferred_element_type=jnp.float32).reshape(
        stream.shape
    )
    stored = (
        normed_one,
        inverse_one,
        acts_one,
        queries,
        extended,
        log_total,
        attended_low,
        normed_two,
        inverse_two,
        acts_two,
        gate_up,
        hidden,
    )
    return (result, stored)


def backward_layer(grad_stream, gathered, stored, cosine, sine, window_mask):
    gain_one, weight_qkv, weight_out, gain_two, weight_in, weight_down = gathered
    (
        normed_one,
        inverse_one,
        acts_one,
        queries,
        extended,
        log_total,
        attended_low,
        normed_two,
        inverse_two,
        acts_two,
        gate_up,
        hidden,
    ) = stored
    sequences, local_length, model_width = grad_stream.shape
    row_count = sequences * local_length
    hidden_units = weight_down.shape[0]
    grad_rows = grad_stream.reshape(row_count, model_width)
    grad_low = grad_rows.astype(jnp.bfloat16)
    down_grad = weight_grad(hidden, grad_low)
    grad_hidden = back_dot(grad_low, weight_down)
    gelu_input = gate_up[:, :hidden_units]
    second = gate_up[:, hidden_units:]
    unused, pull = jax.vjp(lambda a, b: jax.nn.gelu(a, approximate=False) * b, gelu_input, second)
    grad_gelu, grad_second = pull(grad_hidden)
    grad_gate_up = jnp.concatenate([grad_gelu, grad_second], axis=-1).astype(jnp.bfloat16)
    in_grad = weight_grad(acts_two, grad_gate_up)
    grad_acts_two = back_dot(grad_gate_up, weight_in)
    flat_two = normed_two.reshape(row_count, model_width)
    gain_two_grad = jnp.sum(grad_acts_two * flat_two, axis=0)
    grad_middle = grad_rows + norm_back(
        grad_acts_two * gain_two.astype(jnp.float32), flat_two, inverse_two.reshape(row_count, 1)
    )
    grad_middle_low = grad_middle.astype(jnp.bfloat16)
    out_grad = weight_grad(attended_low, grad_middle_low)
    grad_attended = back_dot(grad_middle_low, weight_out).astype(jnp.bfloat16)
    grad_attended = grad_attended.reshape(sequences, local_length, model_width)
    grad_query, grad_pair = attend_back(queries, extended, log_total, grad_attended, window_mask)
    from_next = shifted(grad_pair[:, :HALF].astype(jnp.bfloat16), "shard", -1).astype(jnp.float32)
    from_prior = shifted(
        grad_pair[:, local_length + HALF :].astype(jnp.bfloat16), "shard", 1
    ).astype(jnp.float32)
    middle_part = grad_pair[:, HALF : local_length + HALF]
    middle_part = middle_part.at[:, local_length - HALF :].add(from_next)
    middle_part = middle_part.at[:, :HALF].add(from_prior)
    grad_keys = rotate_back(
        middle_part[..., :model_width].reshape(sequences, local_length, HEADS, HDIM), cosine, sine
    )
    grad_values = middle_part[..., model_width:]
    grad_queries = rotate_back(grad_query, cosine, sine)
    grad_mixed = jnp.concatenate(
        [
            grad_queries.reshape(row_count, model_width),
            grad_keys.reshape(row_count, model_width),
            grad_values.reshape(row_count, model_width),
        ],
        axis=-1,
    ).astype(jnp.bfloat16)
    qkv_grad = weight_grad(acts_one.reshape(row_count, model_width), grad_mixed)
    grad_acts_one = back_dot(grad_mixed, weight_qkv)
    flat_one = normed_one.reshape(row_count, model_width)
    gain_one_grad = jnp.sum(grad_acts_one * flat_one, axis=0)
    grad_input = grad_middle + norm_back(
        grad_acts_one * gain_one.astype(jnp.float32), flat_one, inverse_one.reshape(row_count, 1)
    )
    grad_terms = (gain_one_grad, qkv_grad, out_grad, gain_two_grad, in_grad, down_grad)
    return (grad_input.reshape(grad_stream.shape), grad_terms)


def swap(value, axis):
    return lax.ppermute(value, axis, [(0, 1), (1, 0)])


def swap_z(value, distance):
    count = lax.axis_size("z")
    return lax.ppermute(value, "z", [(i, i ^ distance) for i in range(count)])


def pick(value, index, axis=0):
    return lax.dynamic_index_in_dim(value, index, axis, keepdims=False)


def ordered(index, mine, other, axis=0):
    first = index == 0
    return jnp.stack([jnp.where(first, mine, other), jnp.where(first, other, mine)], axis)


def gather_weight(shard):
    rows, cols = shard.shape
    place_x, place_core, place_y = (lax.axis_index(n) for n in ("x", "core", "shard"))
    mine = pick(shard.reshape(4, rows // 4, cols), place_core * 2 + place_x)
    far = swap(mine, "shard")
    pair = ordered(place_x, far, swap(far, "x")).reshape(rows // 2, cols)
    rest = ordered(place_core, pair, swap(pair, "core")).reshape(rows, cols)
    return ordered(place_y, shard, rest).reshape(2 * rows, cols)


def add_low(left, right):
    return (left.astype(jnp.float32) + right.astype(jnp.float32)).astype(jnp.bfloat16)


def split_add(value, place, send):
    return add_low(pick(value, place), send(pick(value, 1 - place)))


def reduce_chunk(grads):
    _, count, width = grads.shape
    place_x, place_core, place_y, place_z = (
        lax.axis_index(n) for n in ("x", "core", "shard", "z")
    )
    low_z = place_z % 2
    halves = grads.reshape(2, 2, count // 2, width)
    kept = pick(halves, place_core, 1)
    sent = swap(pick(halves, 1 - place_core, 1), "core")
    value = add_low(kept, sent)
    value = split_add(value, place_y, lambda v: swap(v, "shard"))
    value = split_add(value.reshape(2, count // 4, width), place_x, lambda v: swap(v, "x"))
    value = split_add(value.reshape(2, count // 8, width), low_z, lambda v: swap_z(v, 1))
    value = add_low(value, swap_z(value, 2))
    value = ordered(low_z, value, swap_z(value, 1)).reshape(count // 4, width)
    value = ordered(place_x, value, swap(value, "x")).reshape(count // 2, width)
    return ordered(place_core, value, swap(value, "core")).reshape(count, width)


def gain_gather(gain):
    return ordered(lax.axis_index("shard"), gain, swap(gain, "shard"), gain.ndim - 1).reshape(
        gain.shape[:-1] + (2 * gain.shape[-1],)
    )


def by_shard(grad):
    rows, cols = grad.shape
    low = grad.astype(jnp.bfloat16)
    parts = [low[:, n : n + WIDTH].reshape(2, rows // 2, WIDTH) for n in range(0, cols, WIDTH)]
    return parts


def from_shard(value, rows, cols):
    parts = [value[n * rows : (n + 1) * rows] for n in range(cols // WIDTH)]
    return jnp.concatenate(parts, axis=-1).astype(jnp.float32)


def gain_rows(gain, rows):
    return jnp.pad(gain.astype(jnp.bfloat16).reshape(2, 1, WIDTH // 2), ((0, 0), (0, rows - 1), (0, WIDTH // 2)))


WIDTH = 768


def shards_fast(
    tokens, cotangent, gain_attention, heads_in, heads_out, gain_feedforward, expand_in, reduce_out
):
    sequences, local_length, model_width = tokens.shape
    layer_count = heads_in.shape[0]
    offset = lax.axis_index("shard") * local_length
    length_all = local_length * lax.axis_size("shard")
    positions = offset + jnp.arange(local_length, dtype=jnp.int32)
    cosine, sine = rope_tables(positions, HDIM)
    window_mask = build_mask(offset, local_length, length_all)
    gains = gain_gather(jnp.stack([gain_attention, gain_feedforward]))
    kept = []
    for n in range(layer_count):
        kept.append(
            (
                gains[0, n],
                gather_weight(heads_in[n]),
                gather_weight(heads_out[n]),
                gains[1, n],
                gather_weight(expand_in[n]),
                gather_weight(reduce_out[n]),
            )
        )
    stream = tokens.astype(jnp.float32)
    stored_all = []
    for n in range(layer_count):
        stream, stored = forward_layer(stream, kept[n], cosine, sine, window_mask)
        stored_all.append(stored)
    result = stream.astype(jnp.bfloat16)
    grad_stream = cotangent.astype(jnp.float32)
    lists = [None] * layer_count
    for n in reversed(range(layer_count)):
        grad_stream, terms = backward_layer(
            grad_stream, kept[n], stored_all[n], cosine, sine, window_mask
        )
        first = reduce_chunk(
            jnp.concatenate(by_shard(terms[5]) + by_shard(terms[4]) + [gain_rows(terms[3], 64)], 1)
        )
        second = reduce_chunk(
            jnp.concatenate(by_shard(terms[2]) + by_shard(terms[1]) + [gain_rows(terms[0], 128)], 1)
        )
        half, down = WIDTH // 2, reduce_out.shape[1]
        lists[n] = (
            second[4 * half, :half].astype(jnp.float32),
            from_shard(second[half : 4 * half], half, 3 * WIDTH),
            second[:half].astype(jnp.float32),
            first[down + 3 * half, :half].astype(jnp.float32),
            from_shard(first[down : down + 3 * half], half, 3 * WIDTH),
            first[:down].astype(jnp.float32),
        )
    stacked = tuple(jnp.stack([lists[n][k] for n in range(layer_count)]) for k in range(6))
    return (result, grad_stream) + stacked


def shards(
    tokens, cotangent, gain_attention, heads_in, heads_out, gain_feedforward, expand_in, reduce_out
):
    sequences, local_length, model_width = tokens.shape
    layer_count = heads_in.shape[0]
    offset = lax.axis_index("shard") * local_length
    length_all = local_length * lax.axis_size("shard")
    positions = offset + jnp.arange(local_length, dtype=jnp.int32)
    cosine, sine = rope_tables(positions, HDIM)
    window_mask = build_mask(offset, local_length, length_all)
    stream = tokens.astype(jnp.float32)
    kept_weights = []
    stored_all = []
    for layer_num in range(layer_count):
        gathered = (
            lax.all_gather(gain_attention[layer_num], "shard", axis=0, tiled=True),
            lax.all_gather(heads_in[layer_num], "shard", axis=0, tiled=True),
            lax.all_gather(heads_out[layer_num], "shard", axis=0, tiled=True),
            lax.all_gather(gain_feedforward[layer_num], "shard", axis=0, tiled=True),
            lax.all_gather(expand_in[layer_num], "shard", axis=0, tiled=True),
            lax.all_gather(reduce_out[layer_num], "shard", axis=0, tiled=True),
        )
        stream, stored = forward_layer(stream, gathered, cosine, sine, window_mask)
        kept_weights.append(gathered)
        stored_all.append(stored)
    result = stream.astype(jnp.bfloat16)
    grad_stream = cotangent.astype(jnp.float32)
    grad_lists = [None] * layer_count
    for layer_num in reversed(range(layer_count)):
        gathered = (
            lax.all_gather(gain_attention[layer_num], "shard", axis=0, tiled=True),
            lax.all_gather(heads_in[layer_num], "shard", axis=0, tiled=True),
            lax.all_gather(heads_out[layer_num], "shard", axis=0, tiled=True),
            lax.all_gather(gain_feedforward[layer_num], "shard", axis=0, tiled=True),
            lax.all_gather(expand_in[layer_num], "shard", axis=0, tiled=True),
            lax.all_gather(reduce_out[layer_num], "shard", axis=0, tiled=True),
        )
        grad_stream, grad_terms = backward_layer(
            grad_stream, gathered, stored_all[layer_num], cosine, sine, window_mask
        )
        shares = (
            lax.psum_scatter(
                grad_terms[0].astype(jnp.bfloat16), "shard", scatter_dimension=0, tiled=True
            ).astype(jnp.float32),
            lax.psum_scatter(
                grad_terms[1].astype(jnp.bfloat16), "shard", scatter_dimension=0, tiled=True
            ).astype(jnp.float32),
            lax.psum_scatter(
                grad_terms[2].astype(jnp.bfloat16), "shard", scatter_dimension=0, tiled=True
            ).astype(jnp.float32),
            lax.psum_scatter(
                grad_terms[3].astype(jnp.bfloat16), "shard", scatter_dimension=0, tiled=True
            ).astype(jnp.float32),
            lax.psum_scatter(
                grad_terms[4].astype(jnp.bfloat16), "shard", scatter_dimension=0, tiled=True
            ).astype(jnp.float32),
            lax.psum_scatter(
                grad_terms[5].astype(jnp.bfloat16), "shard", scatter_dimension=0, tiled=True
            ).astype(jnp.float32),
        )
        grad_lists[layer_num] = (
            lax.psum(shares[0].astype(jnp.bfloat16), "rep").astype(jnp.float32),
            lax.psum(shares[1].astype(jnp.bfloat16), "rep").astype(jnp.float32),
            lax.psum(shares[2].astype(jnp.bfloat16), "rep").astype(jnp.float32),
            lax.psum(shares[3].astype(jnp.bfloat16), "rep").astype(jnp.float32),
            lax.psum(shares[4].astype(jnp.bfloat16), "rep").astype(jnp.float32),
            lax.psum(shares[5].astype(jnp.bfloat16), "rep").astype(jnp.float32),
        )
    stacked = tuple((jnp.stack([grad_lists[n][k] for n in range(layer_count)]) for k in range(6)))
    return (
        result,
        grad_stream,
        stacked[0],
        stacked[1],
        stacked[2],
        stacked[3],
        stacked[4],
        stacked[5],
    )


def solution(mesh):
    rep, body = "rep", shards
    if mesh.shape["shard"] == 2 and mesh.shape["rep"] == 16:
        rep, body = ("z", "x", "core"), shards_fast
        mesh = Mesh(mesh.devices.reshape(4, 2, 2, 2), ("z", "x", "core", "shard"))
    tokens_spec = P(rep, "shard", None)
    gain_spec = P(None, "shard")
    weight_spec = P(None, "shard", None)
    placed = (gain_spec, weight_spec, weight_spec, gain_spec, weight_spec, weight_spec)
    return jax.shard_map(
        body,
        mesh=mesh,
        in_specs=(tokens_spec, tokens_spec) + placed,
        out_specs=(tokens_spec, tokens_spec) + placed,
        check_vma=False,
    )
```

```python
import math

import jax
import jax.numpy as jnp
from jax import lax
from jax.experimental import pallas as pl
from jax.experimental.pallas import tpu as pltpu
from jax.sharding import Mesh
from jax.sharding import PartitionSpec as P

HEADS = 12
HDIM = 64
HALF = 64
WIDTH = 768

MASKED_SCORE = -1e30
EPSILON = 1e-05


def with_halo(x, sides, width):
    for axis, dim in sides:
        count, length = (lax.axis_size(axis), x.shape[dim])
        up = [(i, (i + 1) % count) for i in range(count - 1)]
        down = [(j, i) for i, j in up]
        last = lax.slice_in_dim(x, length - width, length, axis=dim)
        first = lax.slice_in_dim(x, 0, width, axis=dim)
        before = lax.ppermute(last, axis, up)
        after = lax.ppermute(first, axis, down)
        x = jnp.concatenate([before, x, after], axis=dim)
    return x


def shifted(block, axis, distance):
    devices = range(lax.axis_size(axis))
    route = [(i - distance, i) for i in devices if i - distance in devices]
    return lax.ppermute(block, axis, route)


def normalize(value):
    center = jnp.mean(value, axis=-1, keepdims=True)
    centered = value - center
    inverse = lax.rsqrt(jnp.mean(centered * centered, axis=-1, keepdims=True) + EPSILON)
    return (centered * inverse, inverse)


def norm_back(grad_norm, normed, inverse):
    return inverse * (
        grad_norm
        - jnp.mean(grad_norm, axis=-1, keepdims=True)
        - normed * jnp.mean(grad_norm * normed, axis=-1, keepdims=True)
    )


def rope_tables(positions, head_size):
    half_size = head_size // 2
    freqs = jnp.exp(
        jnp.arange(half_size, dtype=jnp.float32) * (-2.0 * math.log(10000.0) / head_size)
    )
    angles = positions.astype(jnp.float32)[:, None] * freqs[None, :]
    angles = jnp.concatenate([angles, angles], axis=-1)
    return (jnp.cos(angles), jnp.sin(angles))


def rotate(value, cosine, sine):
    half_size = value.shape[-1] // 2
    turned = jnp.concatenate([-value[..., half_size:], value[..., :half_size]], axis=-1)
    return value * cosine[:, None, :] + turned * sine[:, None, :]


def rotate_back(gradient, cosine, sine):
    half_size = gradient.shape[-1] // 2
    scaled = gradient * sine[:, None, :]
    return gradient * cosine[:, None, :] + jnp.concatenate(
        [scaled[..., half_size:], -scaled[..., :half_size]], axis=-1
    )


def into_blocks(extended, block_count, block_rows, key_span):
    return jnp.stack(
        [extended[:, n * block_rows : n * block_rows + key_span] for n in range(block_count)],
        axis=1,
    )


def from_blocks(blocked, block_count, block_rows, key_span, total_rows):
    summed = jnp.zeros(blocked.shape[:1] + (total_rows,) + blocked.shape[3:], blocked.dtype)
    for n in range(block_count):
        summed = summed.at[:, n * block_rows : n * block_rows + key_span].add(blocked[:, n])
    return summed


def build_mask(offset, local_length, length_all):
    block_rows = 2 * HALF
    key_span = 4 * HALF
    block_count = local_length // block_rows
    query_idx = jnp.arange(block_rows, dtype=jnp.int32)[:, None]
    key_idx = jnp.arange(key_span, dtype=jnp.int32)[None, :]
    block_num = jnp.arange(block_count, dtype=jnp.int32)[:, None, None]
    key_pos = offset + block_num * block_rows + key_idx - HALF
    near = jnp.abs(query_idx - key_idx + HALF) <= HALF
    inside = (key_pos >= 0) & (key_pos < length_all)
    return (near & inside)[:, None]


def weight_grad(left, right):
    return lax.dot_general(
        left, right, (((0,), (0,)), ((), ())), preferred_element_type=jnp.float32
    )


def back_dot(gradient, weight):
    return lax.dot_general(
        gradient, weight, (((1,), (1,)), ((), ())), preferred_element_type=jnp.float32
    )


def split_blocks(queries, extended):
    sequences, local_length, head_count, head_size = queries.shape
    model_width = head_count * head_size
    block_rows = 2 * HALF
    key_span = 4 * HALF
    block_count = local_length // block_rows
    query_blocks = queries.reshape(sequences, block_count, block_rows, head_count, head_size)
    key_blocks = into_blocks(extended[..., :model_width], block_count, block_rows, key_span)
    value_blocks = into_blocks(extended[..., model_width:], block_count, block_rows, key_span)
    key_blocks = key_blocks.reshape(sequences, block_count, key_span, head_count, head_size)
    value_blocks = value_blocks.reshape(sequences, block_count, key_span, head_count, head_size)
    return (query_blocks, key_blocks, value_blocks)


def masked_scores(query_blocks, key_blocks, window_mask):
    score_scale = 1.0 / math.sqrt(query_blocks.shape[-1])
    scores = (
        jnp.einsum(
            "snqhd,snkhd->snhqk", query_blocks, key_blocks, preferred_element_type=jnp.float32
        )
        * score_scale
    )
    return jnp.where(window_mask, scores, MASKED_SCORE)


def attend(queries, extended, window_mask):
    sequences, local_length, head_count, head_size = queries.shape
    query_blocks, key_blocks, value_blocks = split_blocks(queries, extended)
    scores = masked_scores(query_blocks, key_blocks, window_mask)
    row_max = jnp.max(scores, axis=-1, keepdims=True)
    exponent = jnp.exp(scores - row_max)
    row_sum = jnp.sum(exponent, axis=-1, keepdims=True)
    probability = (exponent / row_sum).astype(jnp.bfloat16)
    attended = jnp.einsum(
        "snhqk,snkhd->snqhd", probability, value_blocks, preferred_element_type=jnp.float32
    )
    return (
        attended.reshape(sequences, local_length, head_count * head_size),
        row_max + jnp.log(row_sum),
    )


def attend_back(queries, extended, log_total, grad_attended, window_mask):
    sequences, local_length, head_count, head_size = queries.shape
    model_width = head_count * head_size
    block_rows = 2 * HALF
    key_span = 4 * HALF
    block_count = local_length // block_rows
    score_scale = 1.0 / math.sqrt(head_size)
    query_blocks, key_blocks, value_blocks = split_blocks(queries, extended)
    scores = masked_scores(query_blocks, key_blocks, window_mask)
    probability = jnp.exp(scores - log_total)
    grad_blocks = grad_attended.reshape(sequences, block_count, block_rows, head_count, head_size)
    grad_prob = jnp.einsum(
        "snqhd,snkhd->snhqk", grad_blocks, value_blocks, preferred_element_type=jnp.float32
    )
    grad_values = jnp.einsum(
        "snhqk,snqhd->snkhd",
        probability.astype(jnp.bfloat16),
        grad_blocks,
        preferred_element_type=jnp.float32,
    )
    grad_scores = probability * (
        grad_prob - jnp.sum(probability * grad_prob, axis=-1, keepdims=True)
    )
    grad_scores = grad_scores.astype(jnp.bfloat16)
    grad_query = (
        jnp.einsum(
            "snhqk,snkhd->snqhd", grad_scores, key_blocks, preferred_element_type=jnp.float32
        )
        * score_scale
    )
    grad_keys = (
        jnp.einsum(
            "snhqk,snqhd->snkhd", grad_scores, query_blocks, preferred_element_type=jnp.float32
        )
        * score_scale
    )
    joined = jnp.concatenate(
        [
            grad_keys.reshape(sequences, block_count, key_span, model_width),
            grad_values.reshape(sequences, block_count, key_span, model_width),
        ],
        axis=-1,
    )
    grad_pair = from_blocks(joined, block_count, block_rows, key_span, local_length + 2 * HALF)
    return (grad_query.reshape(sequences, local_length, head_count, head_size), grad_pair)


def forward_layer(stream, gathered, cosine, sine, window_mask):
    gain_one, weight_qkv, weight_out, gain_two, weight_in, weight_down = gathered
    sequences, local_length, model_width = stream.shape
    row_count = sequences * local_length
    normed_one, inverse_one = normalize(stream)
    acts_one = (normed_one * gain_one.astype(jnp.float32)).astype(jnp.bfloat16)
    mixed = jnp.dot(
        acts_one.reshape(row_count, model_width), weight_qkv, preferred_element_type=jnp.float32
    )
    mixed = mixed.reshape(sequences, local_length, 3, HEADS, HDIM)
    queries = rotate(mixed[:, :, 0], cosine, sine).astype(jnp.bfloat16)
    key_rows = rotate(mixed[:, :, 1], cosine, sine).astype(jnp.bfloat16)
    value_rows = mixed[:, :, 2].astype(jnp.bfloat16)
    key_value = jnp.concatenate(
        [
            key_rows.reshape(sequences, local_length, model_width),
            value_rows.reshape(sequences, local_length, model_width),
        ],
        axis=-1,
    )
    extended = with_halo(key_value, (("shard", 1),), HALF)
    attended, log_total = attend(queries, extended, window_mask)
    attended_low = attended.astype(jnp.bfloat16).reshape(row_count, model_width)
    middle = stream + jnp.dot(attended_low, weight_out, preferred_element_type=jnp.float32).reshape(
        stream.shape
    )
    normed_two, inverse_two = normalize(middle)
    acts_two = (
        (normed_two * gain_two.astype(jnp.float32))
        .astype(jnp.bfloat16)
        .reshape(row_count, model_width)
    )
    gate_up = jnp.dot(acts_two, weight_in, preferred_element_type=jnp.float32)
    hidden_units = weight_down.shape[0]
    hidden = (
        jax.nn.gelu(gate_up[:, :hidden_units], approximate=False) * gate_up[:, hidden_units:]
    ).astype(jnp.bfloat16)
    result = middle + jnp.dot(hidden, weight_down, preferred_element_type=jnp.float32).reshape(
        stream.shape
    )
    stored = (
        normed_one,
        inverse_one,
        acts_one,
        queries,
        extended,
        log_total,
        attended_low,
        normed_two,
        inverse_two,
        acts_two,
        gate_up,
        hidden,
    )
    return (result, stored)


def backward_layer(grad_stream, gathered, stored, cosine, sine, window_mask):
    gain_one, weight_qkv, weight_out, gain_two, weight_in, weight_down = gathered
    (
        normed_one,
        inverse_one,
        acts_one,
        queries,
        extended,
        log_total,
        attended_low,
        normed_two,
        inverse_two,
        acts_two,
        gate_up,
        hidden,
    ) = stored
    sequences, local_length, model_width = grad_stream.shape
    row_count = sequences * local_length
    hidden_units = weight_down.shape[0]
    grad_rows = grad_stream.reshape(row_count, model_width)
    grad_low = grad_rows.astype(jnp.bfloat16)
    down_grad = weight_grad(hidden, grad_low)
    grad_hidden = back_dot(grad_low, weight_down)
    gelu_input = gate_up[:, :hidden_units]
    second = gate_up[:, hidden_units:]
    unused, pull = jax.vjp(lambda a, b: jax.nn.gelu(a, approximate=False) * b, gelu_input, second)
    grad_gelu, grad_second = pull(grad_hidden)
    grad_gate_up = jnp.concatenate([grad_gelu, grad_second], axis=-1).astype(jnp.bfloat16)
    in_grad = weight_grad(acts_two, grad_gate_up)
    grad_acts_two = back_dot(grad_gate_up, weight_in)
    flat_two = normed_two.reshape(row_count, model_width)
    gain_two_grad = jnp.sum(grad_acts_two * flat_two, axis=0)
    grad_middle = grad_rows + norm_back(
        grad_acts_two * gain_two.astype(jnp.float32), flat_two, inverse_two.reshape(row_count, 1)
    )
    grad_middle_low = grad_middle.astype(jnp.bfloat16)
    out_grad = weight_grad(attended_low, grad_middle_low)
    grad_attended = back_dot(grad_middle_low, weight_out).astype(jnp.bfloat16)
    grad_attended = grad_attended.reshape(sequences, local_length, model_width)
    grad_query, grad_pair = attend_back(queries, extended, log_total, grad_attended, window_mask)
    from_next = shifted(grad_pair[:, :HALF].astype(jnp.bfloat16), "shard", -1).astype(jnp.float32)
    from_prior = shifted(
        grad_pair[:, local_length + HALF :].astype(jnp.bfloat16), "shard", 1
    ).astype(jnp.float32)
    middle_part = grad_pair[:, HALF : local_length + HALF]
    middle_part = middle_part.at[:, local_length - HALF :].add(from_next)
    middle_part = middle_part.at[:, :HALF].add(from_prior)
    grad_keys = rotate_back(
        middle_part[..., :model_width].reshape(sequences, local_length, HEADS, HDIM), cosine, sine
    )
    grad_values = middle_part[..., model_width:]
    grad_queries = rotate_back(grad_query, cosine, sine)
    grad_mixed = jnp.concatenate(
        [
            grad_queries.reshape(row_count, model_width),
            grad_keys.reshape(row_count, model_width),
            grad_values.reshape(row_count, model_width),
        ],
        axis=-1,
    ).astype(jnp.bfloat16)
    qkv_grad = weight_grad(acts_one.reshape(row_count, model_width), grad_mixed)
    grad_acts_one = back_dot(grad_mixed, weight_qkv)
    flat_one = normed_one.reshape(row_count, model_width)
    gain_one_grad = jnp.sum(grad_acts_one * flat_one, axis=0)
    grad_input = grad_middle + norm_back(
        grad_acts_one * gain_one.astype(jnp.float32), flat_one, inverse_one.reshape(row_count, 1)
    )
    grad_terms = (gain_one_grad, qkv_grad, out_grad, gain_two_grad, in_grad, down_grad)
    return (grad_input.reshape(grad_stream.shape), grad_terms)


def shards(
    tokens, cotangent, gain_attention, heads_in, heads_out, gain_feedforward, expand_in, reduce_out
):
    sequences, local_length, model_width = tokens.shape
    layer_count = heads_in.shape[0]
    offset = lax.axis_index("shard") * local_length
    length_all = local_length * lax.axis_size("shard")
    positions = offset + jnp.arange(local_length, dtype=jnp.int32)
    cosine, sine = rope_tables(positions, HDIM)
    window_mask = build_mask(offset, local_length, length_all)
    stream = tokens.astype(jnp.float32)
    kept_weights = []
    stored_all = []
    for layer_num in range(layer_count):
        gathered = (
            lax.all_gather(gain_attention[layer_num], "shard", axis=0, tiled=True),
            lax.all_gather(heads_in[layer_num], "shard", axis=0, tiled=True),
            lax.all_gather(heads_out[layer_num], "shard", axis=0, tiled=True),
            lax.all_gather(gain_feedforward[layer_num], "shard", axis=0, tiled=True),
            lax.all_gather(expand_in[layer_num], "shard", axis=0, tiled=True),
            lax.all_gather(reduce_out[layer_num], "shard", axis=0, tiled=True),
        )
        stream, stored = forward_layer(stream, gathered, cosine, sine, window_mask)
        kept_weights.append(gathered)
        stored_all.append(stored)
    result = stream.astype(jnp.bfloat16)
    grad_stream = cotangent.astype(jnp.float32)
    grad_lists = [None] * layer_count
    for layer_num in reversed(range(layer_count)):
        gathered = (
            lax.all_gather(gain_attention[layer_num], "shard", axis=0, tiled=True),
            lax.all_gather(heads_in[layer_num], "shard", axis=0, tiled=True),
            lax.all_gather(heads_out[layer_num], "shard", axis=0, tiled=True),
            lax.all_gather(gain_feedforward[layer_num], "shard", axis=0, tiled=True),
            lax.all_gather(expand_in[layer_num], "shard", axis=0, tiled=True),
            lax.all_gather(reduce_out[layer_num], "shard", axis=0, tiled=True),
        )
        grad_stream, grad_terms = backward_layer(
            grad_stream, gathered, stored_all[layer_num], cosine, sine, window_mask
        )
        shares = (
            lax.psum_scatter(
                grad_terms[0].astype(jnp.bfloat16), "shard", scatter_dimension=0, tiled=True
            ).astype(jnp.float32),
            lax.psum_scatter(
                grad_terms[1].astype(jnp.bfloat16), "shard", scatter_dimension=0, tiled=True
            ).astype(jnp.float32),
            lax.psum_scatter(
                grad_terms[2].astype(jnp.bfloat16), "shard", scatter_dimension=0, tiled=True
            ).astype(jnp.float32),
            lax.psum_scatter(
                grad_terms[3].astype(jnp.bfloat16), "shard", scatter_dimension=0, tiled=True
            ).astype(jnp.float32),
            lax.psum_scatter(
                grad_terms[4].astype(jnp.bfloat16), "shard", scatter_dimension=0, tiled=True
            ).astype(jnp.float32),
            lax.psum_scatter(
                grad_terms[5].astype(jnp.bfloat16), "shard", scatter_dimension=0, tiled=True
            ).astype(jnp.float32),
        )
        grad_lists[layer_num] = (
            lax.psum(shares[0].astype(jnp.bfloat16), "rep").astype(jnp.float32),
            lax.psum(shares[1].astype(jnp.bfloat16), "rep").astype(jnp.float32),
            lax.psum(shares[2].astype(jnp.bfloat16), "rep").astype(jnp.float32),
            lax.psum(shares[3].astype(jnp.bfloat16), "rep").astype(jnp.float32),
            lax.psum(shares[4].astype(jnp.bfloat16), "rep").astype(jnp.float32),
            lax.psum(shares[5].astype(jnp.bfloat16), "rep").astype(jnp.float32),
        )
    stacked = tuple((jnp.stack([grad_lists[n][k] for n in range(layer_count)]) for k in range(6)))
    return (
        result,
        grad_stream,
        stacked[0],
        stacked[1],
        stacked[2],
        stacked[3],
        stacked[4],
        stacked[5],
    )


ROWS = 128
SPAN = 256
PAIR = 128
NN = (((1,), (0,)), ((), ()))
NT = (((1,), (1,)), ((), ()))
F32 = jnp.float32
LOW = jnp.bfloat16


def dot(left, right, dims=NN):
    return lax.dot_general(left, right, dims, preferred_element_type=F32)


def half_turn(value):
    lane = lax.broadcasted_iota(jnp.int32, value.shape, 1)
    return jnp.where((lane & 63) < 32, pltpu.roll(value, 96, 1), pltpu.roll(value, 32, 1))


def whole(shape):
    return pl.BlockSpec(shape, lambda *at: (0,) * len(shape))


def call(body, grid, ins, outs, scratch, name, operands):
    return pl.pallas_call(
        body,
        grid=grid,
        in_specs=[spec for spec in ins],
        out_specs=[spec for spec, _ in outs],
        out_shape=[shape for _, shape in outs],
        scratch_shapes=scratch,
        compiler_params=pltpu.CompilerParams(
            dimension_semantics=("arbitrary",) * len(grid), vmem_limit_bytes=58 * 1024 * 1024
        ),
        name=name,
    )(*operands)


def out(block, index, shape, dtype):
    return (pl.BlockSpec(block, index), jax.ShapeDtypeStruct(shape, dtype))


def project_body(x_ref, gain_ref, w_ref, cos_ref, sin_ref, qkv_ref, turned_ref, acts):
    step = pl.program_id(0)

    @pl.when(step == 0)
    def _():
        normed, _ = normalize(x_ref[...].astype(F32))
        low = (normed * gain_ref[...].astype(F32)).astype(LOW)
        acts[...] = low
        turned_ref[...] = low.T

    mixed = dot(acts[...], w_ref[...])

    @pl.when(step == 2)
    def _():
        qkv_ref[...] = mixed.astype(LOW)

    @pl.when(step < 2)
    def _():
        scale = jnp.where(step == 0, 0.125, 1.0)
        rows = mixed.shape[0]
        cosine, sine = cos_ref[HALF : HALF + rows], sin_ref[HALF : HALF + rows]
        for at in range(0, WIDTH, PAIR):
            part = mixed[:, at : at + PAIR]
            part = part * cosine + half_turn(part) * sine
            qkv_ref[:, at : at + PAIR] = (part.astype(LOW).astype(F32) * scale).astype(LOW)


def project(x, gain, weight, cosine, sine):
    rows = x.shape[0]
    return call(
        project_body,
        (3,),
        [
            whole((rows, WIDTH)),
            whole((1, WIDTH)),
            pl.BlockSpec((WIDTH, WIDTH), lambda n: (0, n)),
            whole((rows + 2 * HALF, PAIR)),
            whole((rows + 2 * HALF, PAIR)),
        ],
        [
            out((rows, WIDTH), lambda n: (0, n), (rows, 3 * WIDTH), LOW),
            out((WIDTH, rows), lambda n: (0, 0), (WIDTH, rows), LOW),
        ],
        [pltpu.VMEM((rows, WIDTH), LOW)],
        "project",
        (x, gain, weight, cosine, sine),
    )


def fill_window(qkv_ref, before_ref, after_ref, window):
    rows = qkv_ref.shape[0]
    window[:HALF] = before_ref[...]
    window[HALF : HALF + rows] = qkv_ref[:, WIDTH:]
    window[HALF + rows :] = after_ref[...]


def window_bias(block, place, rows, total):
    key = lax.broadcasted_iota(jnp.int32, (SPAN, ROWS), 0)
    query = lax.broadcasted_iota(jnp.int32, (SPAN, ROWS), 1)
    position = place * rows + block * ROWS + key - HALF
    near = jnp.abs(query - key + HALF) <= HALF
    keep = near & (position >= 0) & (position < total)
    bias = jnp.where(keep, 0.0, MASKED_SCORE)
    return jnp.concatenate([bias, bias], axis=1)


def two_heads(pair):
    lane = lax.broadcasted_iota(jnp.int32, pair.shape, 1)
    zero = jnp.zeros_like(pair)
    return jnp.concatenate([jnp.where(lane < HDIM, pair, zero), jnp.where(lane < HDIM, zero, pair)], 0)


def own_blocks(value):
    return jnp.concatenate([value[:HDIM, :ROWS], value[HDIM:, ROWS:]], axis=0)


def attend_body(place_ref, qkv_ref, before_ref, after_ref, o_ref, turned_ref, log_ref, window, *, total):
    block = pl.program_id(0)
    rows = qkv_ref.shape[0]

    @pl.when(block == 0)
    def _():
        fill_window(qkv_ref, before_ref, after_ref, window)

    start = pl.multiple_of(block * ROWS, ROWS)
    bias = window_bias(block, place_ref[0], rows, total)
    for n in range(WIDTH // PAIR):
        lanes = slice(n * PAIR, (n + 1) * PAIR)
        queries = two_heads(qkv_ref[pl.ds(start, ROWS), lanes])
        keys = window[pl.ds(start, SPAN), lanes]
        values = window[pl.ds(start, SPAN), WIDTH + n * PAIR : WIDTH + (n + 1) * PAIR]
        scores = dot(keys, queries, NT) + bias
        top = jnp.max(scores, axis=0, keepdims=True)
        grown = jnp.exp(scores - top)
        summed = jnp.sum(grown, axis=0, keepdims=True)
        chance = (grown * (1.0 / summed)).astype(LOW)
        mixed = own_blocks(dot(values.T, chance)).astype(LOW)
        turned_ref[lanes, :] = mixed
        o_ref[:, lanes] = mixed.T
        log_ref[n : n + 1, :] = (top + jnp.log(summed))


def attend_fwd(place, qkv, before, after, total):
    rows = qkv.shape[0]
    count = rows // ROWS
    pairs = WIDTH // PAIR
    return call(
        lambda *refs: attend_body(*refs, total=total),
        (count,),
        [
            pl.BlockSpec(memory_space=pltpu.SMEM),
            whole((rows, 3 * WIDTH)),
            whole((HALF, 2 * WIDTH)),
            whole((HALF, 2 * WIDTH)),
        ],
        [
            out((ROWS, WIDTH), lambda n: (n, 0), (rows, WIDTH), LOW),
            out((WIDTH, ROWS), lambda n: (0, n), (WIDTH, rows), LOW),
            out((None, 8, SPAN), lambda n: (n, 0, 0), (count, 8, SPAN), F32),
        ],
        [pltpu.VMEM((rows + 2 * HALF, 2 * WIDTH), LOW)],
        "attend",
        (place, qkv, before, after),
    )


def feed_body(x_ref, o_ref, wo_ref, gain_ref, wa_ref, wb_ref, wd_ref,
              mid_ref, turned_ref, hid_ref, left_ref, right_ref, y_ref, acts, total):
    step = pl.program_id(0)

    @pl.when(step == 0)
    def _():
        middle = x_ref[...].astype(F32) + dot(o_ref[...], wo_ref[...])
        mid_ref[...] = middle
        total[...] = middle
        normed, _ = normalize(middle)
        low = (normed * gain_ref[...].astype(F32)).astype(LOW)
        acts[...] = low
        turned_ref[...] = low.T

    first = dot(acts[...], wa_ref[...])
    second = dot(acts[...], wb_ref[...])
    tail = 0.5 * (1.0 + lax.erf(first * (2.0 ** -0.5)))
    bell = jnp.exp(-0.5 * first * first) * ((2.0 * math.pi) ** -0.5)
    gelu = first * tail
    hidden = (gelu * second).astype(LOW)
    hid_ref[...] = hidden.T
    left_ref[...] = (second * (tail + first * bell)).astype(LOW)
    right_ref[...] = gelu.astype(LOW)
    total[...] += dot(hidden, wd_ref[...])

    @pl.when(step == 2)
    def _():
        y_ref[...] = total[...].astype(y_ref.dtype)


def feed(x, o, w_out, gain, w_in, w_down, kind):
    rows = x.shape[0]
    units = w_down.shape[0]
    part = units // 3
    return call(
        feed_body,
        (3,),
        [
            whole((rows, WIDTH)),
            whole((rows, WIDTH)),
            whole((WIDTH, WIDTH)),
            whole((1, WIDTH)),
            pl.BlockSpec((WIDTH, part), lambda n: (0, n)),
            pl.BlockSpec((WIDTH, part), lambda n: (0, n + 3)),
            pl.BlockSpec((part, WIDTH), lambda n: (n, 0)),
        ],
        [
            out((rows, WIDTH), lambda n: (0, 0), (rows, WIDTH), F32),
            out((WIDTH, rows), lambda n: (0, 0), (WIDTH, rows), LOW),
            out((part, rows), lambda n: (n, 0), (units, rows), LOW),
            out((rows, part), lambda n: (0, n), (rows, units), LOW),
            out((rows, part), lambda n: (0, n), (rows, units), LOW),
            out((rows, WIDTH), lambda n: (0, 0), (rows, WIDTH), kind),
        ],
        [pltpu.VMEM((rows, WIDTH), LOW), pltpu.VMEM((rows, WIDTH), F32)],
        "feed",
        (x, o, w_out, gain, w_in, w_in, w_down),
    )


def at_rows(ref, spot):
    shard, row, height = spot
    return ref.at[shard, row : row + height]


def put(source, core_ref, core, kept, sent, spot, sems, slot):
    @pl.when(core_ref[0] == core)
    def _():
        pltpu.make_async_copy(source, at_rows(kept, spot), sems.at[slot]).start()

    @pl.when(core_ref[0] != core)
    def _():
        pltpu.make_async_copy(source, at_rows(sent, spot), sems.at[slot]).start()


def feed_back_body(core_ref, dx_ref, left_ref, right_ref, hid_ref, acts_ref, o_ref, mid_ref, gain_ref,
                   wa_ref, wb_ref, wd_ref, wo_ref, kept_ref, sent_ref, dmid_ref, do_ref, gg_ref,
                   low_dx, total, g_down, g_in, g_out, sems):
    step = pl.program_id(0)
    part = hid_ref.shape[0]
    moved = []

    def ship(source, shard, core, row, size, slot):
        put(source(), core_ref, core, kept_ref, sent_ref, (shard, row, size), sems, slot)
        moved.append((source, shard, row, size, slot))

    @pl.when(step == 0)
    def _():
        low_dx[...] = dx_ref[...].astype(LOW)
        total[...] = jnp.zeros_like(total)

    low = low_dx[...]
    back = dot(low, wd_ref[...], NT)
    first = (back * left_ref[...].astype(F32)).astype(LOW)
    second = (back * right_ref[...].astype(F32)).astype(LOW)
    total[...] += dot(first, wa_ref[...], NT) + dot(second, wb_ref[...], NT)
    g_down[step] = dot(hid_ref[...], low).astype(LOW)
    g_in[step, :, :part] = dot(acts_ref[...], first).astype(LOW)
    g_in[step, :, part:] = dot(acts_ref[...], second).astype(LOW)
    size = WIDTH // 4
    for n in range(3):

        @pl.when(step == n)
        def _():
            for piece in range(part // 96):
                at = n * (part // 96) + piece
                owner, inner = at // 3, at % 3
                ship(
                    lambda n=n, row=piece * 96: g_down.at[n, row : row + 96],
                    owner // 2,
                    owner % 2,
                    inner * 96,
                    96,
                    at,
                )
            for owner in range(4):
                ship(
                    lambda n=n, row=owner * size: g_in.at[n, row : row + size],
                    owner // 2,
                    owner % 2,
                    3 * 96 + n * size,
                    size,
                    12 + 4 * n + owner,
                )

    @pl.when(step == 2)
    def _():
        grad_acts = total[...]
        normed, inverse = normalize(mid_ref[...])
        gg_ref[...] = jnp.sum(grad_acts * normed, axis=0, keepdims=True)
        grad_mid = dx_ref[...].astype(F32) + norm_back(
            grad_acts * gain_ref[...].astype(F32), normed, inverse
        )
        dmid_ref[...] = grad_mid
        low_mid = grad_mid.astype(LOW)
        do_ref[...] = dot(low_mid, wo_ref[...], NT).astype(LOW)
        g_out[...] = dot(o_ref[...], low_mid).astype(LOW)
        for owner in range(4):
            ship(
                lambda row=owner * size: g_out.at[row : row + size],
                owner // 2,
                owner % 2,
                3 * 96 + 3 * size,
                size,
                24 + owner,
            )
        for source, shard, row, height, slot in moved:
            spot = (shard, row, height)
            pltpu.make_async_copy(source(), at_rows(kept_ref, spot), sems.at[slot]).wait()


def feed_back(core, dx, left, right, hid, acts, o, mid, gain, w_in, w_down, w_out):
    rows = dx.shape[0]
    units = w_down.shape[0]
    part = units // 3
    count = units // 4 + WIDTH
    held = jax.ShapeDtypeStruct((2, count, WIDTH), LOW)
    return call(
        feed_back_body,
        (3,),
        [
            pl.BlockSpec(memory_space=pltpu.SMEM),
            whole((rows, WIDTH)),
            pl.BlockSpec((rows, part), lambda n: (0, n)),
            pl.BlockSpec((rows, part), lambda n: (0, n)),
            pl.BlockSpec((part, rows), lambda n: (n, 0)),
            whole((WIDTH, rows)),
            whole((WIDTH, rows)),
            whole((rows, WIDTH)),
            whole((1, WIDTH)),
            pl.BlockSpec((WIDTH, part), lambda n: (0, n)),
            pl.BlockSpec((WIDTH, part), lambda n: (0, n + 3)),
            pl.BlockSpec((part, WIDTH), lambda n: (n, 0)),
            whole((WIDTH, WIDTH)),
        ],
        [
            (pl.BlockSpec(memory_space=pl.ANY), held),
            (pl.BlockSpec(memory_space=pl.ANY), held),
            out((rows, WIDTH), lambda n: (0, 0), (rows, WIDTH), F32),
            out((rows, WIDTH), lambda n: (0, 0), (rows, WIDTH), LOW),
            out((1, WIDTH), lambda n: (0, 0), (1, WIDTH), F32),
        ],
        [
            pltpu.VMEM((rows, WIDTH), LOW),
            pltpu.VMEM((rows, WIDTH), F32),
            pltpu.VMEM((3, part, WIDTH), LOW),
            pltpu.VMEM((3, WIDTH, WIDTH), LOW),
            pltpu.VMEM((WIDTH, WIDTH), LOW),
            pltpu.SemaphoreType.DMA((28,)),
        ],
        "feed_back",
        (core, dx, left, right, hid, acts, o, mid, gain, w_in, w_in, w_down, w_out),
    )


def attend_back_body(place_ref, qkv_ref, before_ref, after_ref, log_ref, do_ref, cos_ref, sin_ref,
                     dqkv_ref, edge_ref, window, sums, *, total):
    block = pl.program_id(0)
    rows = qkv_ref.shape[0]
    count = pl.num_programs(0)

    @pl.when(block == 0)
    def _():
        fill_window(qkv_ref, before_ref, after_ref, window)
        sums[...] = jnp.zeros_like(sums)

    start = pl.multiple_of(block * ROWS, ROWS)
    bias = window_bias(block, place_ref[0], rows, total)
    cosine = cos_ref[pl.ds(start + HALF, ROWS), :]
    sine = sin_ref[pl.ds(start + HALF, ROWS), :]
    for n in range(WIDTH // PAIR):
        lanes = slice(n * PAIR, (n + 1) * PAIR)
        more = slice(WIDTH + n * PAIR, WIDTH + (n + 1) * PAIR)
        queries = two_heads(qkv_ref[pl.ds(start, ROWS), lanes])
        grads = two_heads(do_ref[:, lanes])
        keys = window[pl.ds(start, SPAN), lanes]
        values = window[pl.ds(start, SPAN), more]
        scores = dot(keys, queries, NT) + bias
        chance = jnp.exp(scores - log_ref[n : n + 1, :])
        grad_chance = dot(values, grads, NT)
        sums[pl.ds(start, SPAN), more] += dot(chance.astype(LOW), grads)
        inner = jnp.sum(chance * grad_chance, axis=0, keepdims=True)
        grad_scores = (chance * (grad_chance - inner)).astype(LOW)
        sums[pl.ds(start, SPAN), lanes] += dot(grad_scores, queries)
        grad_query = own_blocks(dot(keys.T, grad_scores)).T * 0.125
        grad_query = grad_query * cosine - half_turn(grad_query) * sine
        dqkv_ref[pl.ds(start, ROWS), lanes] = grad_query.astype(LOW)

    @pl.when(block == count - 1)
    def _():
        for n in range(WIDTH // PAIR):
            lanes = slice(n * PAIR, (n + 1) * PAIR)
            more = slice(WIDTH + n * PAIR, WIDTH + (n + 1) * PAIR)
            turned = sums[:, lanes]
            turned = (turned * cos_ref[...] - half_turn(turned) * sin_ref[...]).astype(LOW)
            plain = sums[:, more].astype(LOW)
            edge_ref[0, :, lanes] = turned[:HALF]
            edge_ref[1, :, lanes] = turned[HALF + rows :]
            edge_ref[0, :, more] = plain[:HALF]
            edge_ref[1, :, more] = plain[HALF + rows :]
            dqkv_ref[:, more] = turned[HALF : HALF + rows]
            dqkv_ref[:, 2 * WIDTH + n * PAIR : 2 * WIDTH + (n + 1) * PAIR] = plain[HALF : HALF + rows]


def attend_bwd(place, qkv, before, after, logs, do, cosine, sine, total):
    rows = qkv.shape[0]
    count = rows // ROWS
    wide = rows + 2 * HALF
    return call(
        lambda *refs: attend_back_body(*refs, total=total),
        (count,),
        [
            pl.BlockSpec(memory_space=pltpu.SMEM),
            whole((rows, 3 * WIDTH)),
            whole((HALF, 2 * WIDTH)),
            whole((HALF, 2 * WIDTH)),
            pl.BlockSpec((None, 8, SPAN), lambda n: (n, 0, 0)),
            pl.BlockSpec((ROWS, WIDTH), lambda n: (n, 0)),
            whole((wide, PAIR)),
            whole((wide, PAIR)),
        ],
        [
            out((rows, 3 * WIDTH), lambda n: (0, 0), (rows, 3 * WIDTH), LOW),
            out((2, HALF, 2 * WIDTH), lambda n: (0, 0, 0), (2, HALF, 2 * WIDTH), LOW),
        ],
        [pltpu.VMEM((wide, 2 * WIDTH), LOW), pltpu.VMEM((wide, 2 * WIDTH), F32)],
        "attend_back",
        (place, qkv, before, after, logs, do, cosine, sine),
    )


def project_back_body(core_ref, place_ref, dqkv_ref, edge_ref, acts_ref, x_ref, gain_ref, w_ref, dmid_ref, more_ref,
                      kept_ref, sent_ref, dx_ref, gg_ref, total, grads, g_w, g_gain, sems, *, pad):
    step = pl.program_id(0)
    rows = dqkv_ref.shape[0]
    size = WIDTH // 4
    moved = []

    def ship(source, shard, core, row, height, slot):
        put(source(), core_ref, core, kept_ref, sent_ref, (shard, row, height), sems, slot)
        moved.append((source, shard, row, height, slot))

    grads[...] = dqkv_ref[...]

    @pl.when((step > 0) & (place_ref[0] == 0))
    def _():
        tail = slice(rows - HALF, rows)
        grads[tail] = (dqkv_ref[tail].astype(F32) + edge_ref[...].astype(F32)).astype(LOW)

    @pl.when((step > 0) & (place_ref[0] == 1))
    def _():
        grads[:HALF] = (dqkv_ref[:HALF].astype(F32) + edge_ref[...].astype(F32)).astype(LOW)

    part = dot(grads[...], w_ref[...], NT)

    @pl.when(step == 0)
    def _():
        total[...] = part

    @pl.when(step > 0)
    def _():
        total[...] += part

    g_w[step] = dot(acts_ref[...], grads[...]).astype(LOW)
    for n in range(3):

        @pl.when(step == n)
        def _():
            for owner in range(4):
                ship(
                    lambda n=n, row=owner * size: g_w.at[n, row : row + size],
                    owner // 2,
                    owner % 2,
                    n * size,
                    size,
                    4 * n + owner,
                )

    @pl.when(step == 2)
    def _():
        grad_acts = total[...]
        normed, inverse = normalize(x_ref[...].astype(F32))
        gain_grad = jnp.sum(grad_acts * normed, axis=0, keepdims=True)
        gg_ref[...] = gain_grad
        dx_ref[...] = dmid_ref[...] + norm_back(grad_acts * gain_ref[...].astype(F32), normed, inverse)
        if pad:
            everything = jnp.concatenate(
                [more_ref[...], gain_grad, jnp.zeros((pad - 1 - more_ref.shape[0], WIDTH), F32)], 0
            ).astype(LOW)
            for owner in range(4):
                g_gain[owner] = jnp.where(owner % 2 == 0, everything, jnp.zeros_like(everything))
            for owner in range(4):
                ship(lambda owner=owner: g_gain.at[owner], owner // 2, owner % 2, 3 * size, pad, 12 + owner)
        for source, shard, row, height, slot in moved:
            spot = (shard, row, height)
            pltpu.make_async_copy(source(), at_rows(kept_ref, spot), sems.at[slot]).wait()


def project_back(core, place, dqkv, edge, acts, x, gain, weight, dmid, more, pad):
    rows = x.shape[0]
    held = jax.ShapeDtypeStruct((2, 3 * WIDTH // 4 + pad, WIDTH), LOW)
    return call(
        lambda *refs: project_back_body(*refs, pad=pad),
        (3,),
        [
            pl.BlockSpec(memory_space=pltpu.SMEM),
            pl.BlockSpec(memory_space=pltpu.SMEM),
            pl.BlockSpec((rows, WIDTH), lambda n: (0, n)),
            pl.BlockSpec((HALF, WIDTH), lambda n: (0, jnp.maximum(n - 1, 0))),
            whole((WIDTH, rows)),
            whole((rows, WIDTH)),
            whole((1, WIDTH)),
            pl.BlockSpec((WIDTH, WIDTH), lambda n: (0, n)),
            whole((rows, WIDTH)),
            whole(more.shape),
        ],
        [
            (pl.BlockSpec(memory_space=pl.ANY), held),
            (pl.BlockSpec(memory_space=pl.ANY), held),
            out((rows, WIDTH), lambda n: (0, 0), (rows, WIDTH), F32),
            out((1, WIDTH), lambda n: (0, 0), (1, WIDTH), F32),
        ],
        [
            pltpu.VMEM((rows, WIDTH), F32),
            pltpu.VMEM((rows, WIDTH), LOW),
            pltpu.VMEM((3, WIDTH, WIDTH), LOW),
            pltpu.VMEM((4, max(pad, 8), WIDTH), LOW),
            pltpu.SemaphoreType.DMA((16,)),
        ],
        "project_back",
        (core, place, dqkv, edge, acts, x, gain, weight, dmid, more),
    )


def swap(value, axis):
    return lax.ppermute(value, axis, [(0, 1), (1, 0)])


def swap_z(value, distance):
    count = lax.axis_size("z")
    return lax.ppermute(value, "z", [(i, i ^ distance) for i in range(count)])


def pick(value, index, axis=0):
    return lax.dynamic_index_in_dim(value, index, axis, keepdims=False)


def ordered(index, mine, other, axis=0):
    first = index == 0
    return jnp.stack([jnp.where(first, mine, other), jnp.where(first, other, mine)], axis)


def gather_weight(shard):
    rows, cols = shard.shape
    place_x, place_core, place_y = (lax.axis_index(n) for n in ("x", "core", "shard"))
    mine = pick(shard.reshape(4, rows // 4, cols), place_core * 2 + place_x)
    far = swap(mine, "shard")
    pair = ordered(place_x, far, swap(far, "x")).reshape(rows // 2, cols)
    rest = ordered(place_core, pair, swap(pair, "core")).reshape(rows, cols)
    return ordered(place_y, shard, rest).reshape(2 * rows, cols)


def add_low(left, right):
    return (left.astype(F32) + right.astype(F32)).astype(LOW)


def split_add(value, place, send):
    return add_low(pick(value, place), send(pick(value, 1 - place)))


def reduce_chunk(kept, sent):
    _, count, width = kept.shape
    place_x, place_core, place_y, place_z = (
        lax.axis_index(n) for n in ("x", "core", "shard", "z")
    )
    low_z = place_z % 2
    value = add_low(kept, swap(sent, "core"))
    value = split_add(value, place_y, lambda v: swap(v, "shard"))
    value = split_add(value.reshape(2, count // 2, width), place_x, lambda v: swap(v, "x"))
    value = split_add(value.reshape(2, count // 4, width), low_z, lambda v: swap_z(v, 1))
    value = add_low(value, swap_z(value, 2))
    value = ordered(low_z, value, swap_z(value, 1)).reshape(count // 2, width)
    value = ordered(place_x, value, swap(value, "x")).reshape(count, width)
    return ordered(place_core, value, swap(value, "core"))


def pieces(value, start, size, width=WIDTH):
    return value[:, start : start + size].reshape(2 * size, width)


def shards_fast(
    tokens, cotangent, gain_attention, heads_in, heads_out, gain_feedforward, expand_in, reduce_out
):
    _, rows, _ = tokens.shape
    layer_count = heads_in.shape[0]
    place_y, place_core = lax.axis_index("shard"), lax.axis_index("core")
    total = rows * lax.axis_size("shard")
    place, core = (v.astype(jnp.int32).reshape(1) for v in (place_y, place_core))
    positions = place_y * rows - HALF + jnp.arange(rows + 2 * HALF, dtype=jnp.int32)
    cosine, sine = rope_tables(positions, HDIM)
    sign = jnp.where(jnp.arange(PAIR) % HDIM < HDIM // 2, -1.0, 1.0).astype(F32)
    cosine = jnp.concatenate([cosine, cosine], axis=1)
    sine = jnp.concatenate([sine, sine], axis=1) * sign
    shares = jnp.stack([gain_attention, gain_feedforward])
    gains = ordered(place_y, shares, swap(shares, "shard"), 2).reshape(2, layer_count, 1, WIDTH)
    kept = []
    for n in range(layer_count):
        kept.append(
            (
                gather_weight(heads_in[n]),
                gather_weight(heads_out[n]),
                gather_weight(expand_in[n]),
                gather_weight(reduce_out[n]),
            )
        )
    stream = tokens.reshape(rows, WIDTH)
    stored = []
    for n in range(layer_count):
        w_heads, w_out, w_in, w_down = kept[n]
        qkv, acts_one = project(stream, gains[0, n], w_heads, cosine, sine)
        edge = jnp.where(place_y == 0, qkv[rows - HALF :, WIDTH:], qkv[:HALF, WIDTH:])
        edge = swap(edge, "shard")
        o, o_turned, logs = attend_fwd(place, qkv, edge, edge, total)
        kind = LOW if n == layer_count - 1 else F32
        middle, acts_two, hidden, left, right, after = feed(
            stream, o, w_out, gains[1, n], w_in, w_down, kind
        )
        stored.append((stream, qkv, acts_one, edge, o_turned, logs, middle, acts_two, hidden, left, right))
        stream = after
    result = stream.reshape(tokens.shape)
    grad = cotangent.reshape(rows, WIDTH)
    gain_grads = []
    sums = [None] * layer_count
    for n in reversed(range(layer_count)):
        w_heads, w_out, w_in, w_down = kept[n]
        before, qkv, acts_one, edge, o_turned, logs, middle, acts_two, hidden, left, right = stored[n]
        held, sent, grad_mid, do, gain_two = feed_back(
            core, grad, left, right, hidden, acts_two, o_turned, middle, gains[1, n], w_in, w_down, w_out
        )
        gain_grads.append(gain_two)
        first = reduce_chunk(held, sent)
        grad_qkv, edges = attend_bwd(place, qkv, edge, edge, logs, do, cosine, sine, total)
        moved = swap(pick(edges, 1 - place_y), "shard")
        pad = 32 if n == 0 else 0
        more = jnp.concatenate(gain_grads, axis=0)
        held, sent, grad, gain_one = project_back(
            core, place, grad_qkv, moved, acts_one, before, gains[0, n], w_heads, grad_mid, more, pad
        )
        gain_grads.append(gain_one)
        sums[n] = (first, reduce_chunk(held, sent))
    half, quarter, third, down = WIDTH // 2, WIDTH // 4, reduce_out.shape[1] // 2, reduce_out.shape[1]
    lists = []
    rows_at = 3 * quarter
    for n in range(layer_count):
        first, second = sums[n]
        heads = jnp.concatenate([pieces(second, k * quarter, quarter) for k in range(3)], 1)
        spread = [pieces(first, third + k * quarter, quarter) for k in range(3)]
        expand = jnp.concatenate([v[:, :half] for v in spread] + [v[:, half:] for v in spread], 1)
        at = 2 * (layer_count - 1 - n)
        gain_two, gain_one = (
            lax.dynamic_slice_in_dim(sums[0][1][0, rows_at + k], place_y * half, half) for k in (at, at + 1)
        )
        lists.append(
            (
                gain_one,
                heads,
                pieces(first, third + 3 * quarter, quarter),
                gain_two,
                expand,
                pieces(first, 0, third),
            )
        )
    stacked = tuple(
        jnp.stack([lists[n][k].astype(F32) for n in range(layer_count)]) for k in range(6)
    )
    return (result, grad.reshape(tokens.shape)) + stacked


def solution(mesh):
    rep, body = "rep", shards
    if mesh.shape["shard"] == 2 and mesh.shape["rep"] == 16:
        rep, body = ("z", "x", "core"), shards_fast
        mesh = Mesh(mesh.devices.reshape(4, 2, 2, 2), ("z", "x", "core", "shard"))
    tokens_spec = P(rep, "shard", None)
    gain_spec = P(None, "shard")
    weight_spec = P(None, "shard", None)
    placed = (gain_spec, weight_spec, weight_spec, gain_spec, weight_spec, weight_spec)
    return jax.shard_map(
        body,
        mesh=mesh,
        in_specs=(tokens_spec, tokens_spec) + placed,
        out_specs=(tokens_spec, tokens_spec) + placed,
        check_vma=False,
    )
```
